32 devices in a mesh: dp: 8 (over z, x), tensor: 4 (over y, core).
Axes of the slice: x: 2, y: 2, z: 4, core: 2. Of those that a mesh axis runs over, the one named last changes fastest.
Arguments:
- momentum: float32 [8, 8192, 1024], P('dp', None, 'tensor'), may hold values from -6 to 6
- gradient: bfloat16 [8, 8192, 1024], P('dp', None, 'tensor'), may hold values from -6 to 6
- masters: float32 [8192, 1024], P('dp', 'tensor'), may hold values from -6 to 6
- tokens: bfloat16 [1024, 8192], P('dp', 'tensor'), may hold values from -6 to 6
- freq_index: int32 [8, 1024], P('tensor'), may hold values from 0 to 8191, as said below
Outputs:
- residual: float32 [8, 8192, 1024], P('dp', None, 'tensor')
- new_masters: float32 [8192, 1024], P('dp', 'tensor')
- keys_out: bfloat16 [1024, 1024], P('dp', 'tensor')
The draws below stay inside these ranges and needn't reach their ends.
Inputs may be any that keep to these rules, and one draw needn't show every extreme that they name: `freq_index`: each row lists 1024 distinct frequencies, 0 and 8191 among them; the same list serves every replica.
All inputs are finite; a program needn't handle non-finite values.
Results may differ from the reference program's by a relative error of at most 0.007.
Values may be sent and summed in bfloat16 or wider, within the bound.
No kernel may reach another device: no remote copies, remote signals or barrier semaphores. Data moves between devices by JAX's collectives and lax.ppermute only.
A program may use at most 128 MiB of HBM per device.

```python
import math
import jax
import jax.numpy as jnp
from jax import lax

D = 8192
COLS = 1024
CB = 128
FREQS = 1024
BLOCKS = 8
REPLICAS = 8
TOKENS = 1024


def draw_freq_index(key, part):
    keys = jax.random.split(key, BLOCKS)

    def one_block(block_key):
        pick_key, order_key = jax.random.split(block_key)
        chosen = jax.random.permutation(pick_key, D - 2)[:FREQS - 2] + 1
        listed = jnp.concatenate([jnp.array([0, D - 1], jnp.int32), chosen.astype(jnp.int32)])
        return listed[jax.random.permutation(order_key, FREQS)]
    return jax.vmap(one_block)(keys)


def steps_of(stream_key, shape, pieces, least, top_value):
    gain = 1.0
    for dim, blocks in pieces:
        steps = jax.random.uniform(jax.random.fold_in(jax.random.fold_in(stream_key, 6), dim), (blocks,), jnp.float32, least / len(pieces), top_value / len(pieces))
        gain = gain * jnp.repeat(jnp.exp(steps), shape[dim] // blocks).reshape((-1,) + (1,) * (len(shape) - 1 - dim))
    return gain


def normal_values(stream_key, shape, scale, limit, cuts=(), kind=jnp.bfloat16):
    entries = jax.random.normal(stream_key, shape, jnp.float32) * scale
    if len(cuts) > 0:
        entries = steps_of(stream_key, shape, cuts, -0.22, 0.18) * entries
    return jnp.clip(entries, min=-limit, max=limit).astype(kind)


def setup_inputs(seed: int = 0) -> dict:
    streams_of = jax.random.split(jax.random.key(seed), 6)
    momentum = normal_values(streams_of[0], (REPLICAS, D, COLS), 1.0, 6.0, ((0, 8), (2, 4)), jnp.float32)
    gradient = normal_values(streams_of[1], (REPLICAS, D, COLS), 1.0, 6.0, ((0, 8), (2, 4)))
    masters = normal_values(streams_of[2], (D, COLS), 1.0, 6.0, ((0, 8), (1, 4)), jnp.float32)
    tokens = normal_values(streams_of[3], (TOKENS, D), 1.0, 6.0, ((0, 8), (1, 4)))
    freq_index = draw_freq_index(jax.random.fold_in(streams_of[5], 71), 0)
    return {"momentum": momentum, "gradient": gradient, "masters": masters, "tokens": tokens, "freq_index": freq_index}


momentum_decay = 0.9
step_rate = 1.0

def cosine_rows(frequency, first_row, row_count, model_width):
    positions = first_row + lax.iota(jnp.int32, row_count)
    phases = (2 * positions + 1)[None, :] * frequency[:, None] % (4 * model_width)
    angles = phases.astype(jnp.float32) * (math.pi / (2 * model_width))
    scales = jnp.where(frequency == 0, math.sqrt(1.0 / model_width), math.sqrt(2.0 / model_width)).astype(jnp.float32)
    return (scales[:, None] * jnp.cos(angles)).astype(jnp.bfloat16)

def reference(momentum, gradient, masters, tokens, freq_index):
    replicas = momentum.shape[0]
    remains = []
    updates = []
    highest = lax.Precision.HIGHEST
    for column_block in range(COLS // CB):
        lower = column_block * CB
        cosines = cosine_rows(freq_index[column_block], 0, D, D)

        def replica_step(summed, inputs):
            moment_rows, grad_rows = inputs
            states = momentum_decay * moment_rows + grad_rows.astype(jnp.float32)
            coefficient = jnp.dot(cosines, states.astype(jnp.bfloat16), preferred_element_type=jnp.float32).astype(jnp.bfloat16)
            remain = states - jnp.dot(cosines.T, coefficient, preferred_element_type=jnp.float32)
            return (summed + coefficient.astype(jnp.float32), remain)
        summed, remain = lax.scan(replica_step, jnp.zeros((FREQS, CB), jnp.float32), (momentum[:, :, lower:lower + CB], gradient[:, :, lower:lower + CB]))
        remains.append(remain)
        updates.append(jnp.dot(cosines.astype(jnp.float32).T, summed / replicas, precision=highest))
    residual = jnp.concatenate(remains, axis=2)
    update = jnp.concatenate(updates, axis=1)
    new_masters = masters - step_rate * update
    weights = new_masters.astype(jnp.bfloat16)
    projected = jnp.dot(tokens, weights, preferred_element_type=jnp.float32) * D ** (-0.5)
    return (residual, new_masters, projected.astype(jnp.bfloat16))
```

```python
import math

import jax
import jax.numpy as jnp
from jax import lax
from jax.experimental import pallas as pl
from jax.experimental.pallas import tpu as pltpu
from jax.sharding import PartitionSpec as P

momentum_decay = 0.9
step_rate = 1.0
fine_rows = 64
flip_rows = 128
f32 = jnp.float32
bf16 = jnp.bfloat16


def sine_cosine(phase, model_width):
    quarter = (phase + model_width // 2) // model_width
    x = (phase - quarter * model_width).astype(f32) * (math.pi / (2 * model_width))
    z = x * x
    sine = x + x * z * (-1.6666654611e-1 + z * (8.3321608736e-3 + z * -1.9515295891e-4))
    cosine = 1.0 - 0.5 * z + z * z * (
        4.166664568298827e-2 + z * (-1.388731625493765e-3 + z * 2.443315711809948e-5)
    )
    swapped = (quarter & 1) == 1
    cos_sign = jnp.where(((quarter + 1) & 2) == 2, -1.0, 1.0).astype(f32)
    sin_sign = jnp.where((quarter & 2) == 2, -1.0, 1.0).astype(f32)
    return (
        cos_sign * jnp.where(swapped, sine, cosine),
        sin_sign * jnp.where(swapped, cosine, sine),
    )


def fill_tables(frequency, first_row, coarse_cos, coarse_sin, fine_cos, fine_sin, model_width):
    period = 4 * model_width
    freqs = frequency.shape[1]
    coarse = lax.broadcasted_iota(jnp.int32, (coarse_cos.shape[0], freqs), 0)
    fine = lax.broadcasted_iota(jnp.int32, (fine_rows, freqs), 0)
    scale = jnp.where(
        frequency == 0, math.sqrt(1.0 / model_width), math.sqrt(2.0 / model_width)
    ).astype(f32)
    cosine, sine = sine_cosine(
        (2 * (first_row + coarse * fine_rows)) * frequency % period, model_width
    )
    coarse_cos[...] = cosine * scale
    coarse_sin[...] = sine * scale
    cosine, sine = sine_cosine((2 * fine + 1) * frequency % period, model_width)
    fine_cos[...] = cosine
    fine_sin[...] = sine


def fill_cosines(target, first_coarse, count, coarse_cos, coarse_sin, fine_cos, fine_sin):
    for lane in range(0, target.shape[1], 128):
        lanes = pl.ds(lane, 128)
        cosine = fine_cos[:, lanes]
        sine = fine_sin[:, lanes]
        coarse_c = coarse_cos[pl.ds(first_coarse, count), lanes]
        coarse_s = coarse_sin[pl.ds(first_coarse, count), lanes]
        for k in range(count):
            target[pl.ds(k * fine_rows, fine_rows), lanes] = (
                coarse_c[k : k + 1] * cosine - coarse_s[k : k + 1] * sine
            ).astype(bf16)


def reversal():
    rows = lax.broadcasted_iota(jnp.int32, (flip_rows, flip_rows), 0)
    cols = lax.broadcasted_iota(jnp.int32, (flip_rows, flip_rows), 1)
    return jnp.where(rows + cols == flip_rows - 1, 1.0, 0.0).astype(bf16)


def flip_low(value):
    flips = reversal()
    pieces = [
        jnp.dot(flips, value[lower : lower + flip_rows], preferred_element_type=f32)
        for lower in range(value.shape[0] - flip_rows, -1, -flip_rows)
    ]
    return jnp.concatenate(pieces, axis=0)


def flip_wide(value):
    high = value.astype(bf16)
    low = (value - high.astype(f32)).astype(bf16)
    return flip_low(high) + flip_low(low)


def parity_sign(frequency):
    return (1 - 2 * (frequency & 1)).astype(f32)


def dot_tn(a, b):
    return lax.dot_general(a, b, (((0,), (0,)), ((), ())), preferred_element_type=f32)


def dot_nt(a, b):
    return lax.dot_general(a, b, (((1,), (1,)), ((), ())), preferred_element_type=f32)


def forward(column_block, momentum, gradient, freq_rows, meta, group):
    model_width = momentum.shape[1]
    block_cols = momentum.shape[2] // freq_rows.shape[0]
    freqs = freq_rows.shape[2]
    half = model_width // 2
    tile = min(512, half)
    steps = half // tile
    piece = block_cols // group

    def kernel(meta_ref, freq, mom_a, mom_b, grad_a, grad_b, coeff, *rest):
        pieces = rest[:group]
        table, total, coarse_cos, coarse_sin, fine_cos, fine_sin = rest[group:]
        step = pl.program_id(0)
        frequency = freq[0]

        @pl.when(step == 0)
        def _():
            fill_tables(frequency, 0, coarse_cos, coarse_sin, fine_cos, fine_sin, model_width)

        fill_cosines(
            table, pl.multiple_of(step * (tile // fine_rows), tile // fine_rows),
            tile // fine_rows,
            coarse_cos, coarse_sin, fine_cos, fine_sin,
        )
        low_a = (momentum_decay * mom_a[0] + grad_a[0].astype(f32)).astype(bf16)
        low_b = (momentum_decay * mom_b[0] + grad_b[0].astype(f32)).astype(bf16)
        both = jnp.concatenate([low_a, flip_low(low_b).astype(bf16)], axis=1)
        partial = dot_tn(both, table[...])

        @pl.when(step == 0)
        def _():
            total[...] = partial

        @pl.when(step > 0)
        def _():
            total[...] += partial

        @pl.when(step == steps - 1)
        def _():
            coeff[...] = (
                total[:block_cols] + parity_sign(frequency) * total[block_cols:]
            ).astype(bf16)
            for k in range(group):
                start = ((meta_ref[0] % group) ^ k) * piece
                pieces[k][...] = coeff[pl.ds(pl.multiple_of(start, piece), piece), :]

    def rows(which):
        def index(step, meta_ref):
            return (0, 2 * steps - 1 - step if which else step, column_block)

        return pl.BlockSpec((1, tile, block_cols), index)

    whole = lambda step, meta_ref: (0, 0)
    return pl.pallas_call(
        kernel,
        name=f"forward_{column_block}",
        grid_spec=pltpu.PrefetchScalarGridSpec(
            num_scalar_prefetch=1,
            grid=(steps,),
            in_specs=[
                pl.BlockSpec((1, 1, freqs), lambda step, meta_ref: (column_block, 0, 0)),
                rows(0), rows(1), rows(0), rows(1),
            ],
            out_specs=[pl.BlockSpec((block_cols, freqs), whole)]
            + [pl.BlockSpec((piece, freqs), whole)] * group
            + [pl.BlockSpec((tile, freqs), lambda step, meta_ref: (step, 0))],
            scratch_shapes=[pltpu.VMEM((2 * block_cols, freqs), f32)]
            + [pltpu.VMEM((half // fine_rows, freqs), f32)] * 2
            + [pltpu.VMEM((fine_rows, freqs), f32)] * 2,
        ),
        out_shape=[jax.ShapeDtypeStruct((block_cols, freqs), bf16)]
        + [jax.ShapeDtypeStruct((piece, freqs), bf16)] * group
        + [jax.ShapeDtypeStruct((half, freqs), bf16)],
    )(meta, freq_rows, momentum, momentum, gradient, gradient)


def remain(column_block, momentum, gradient, freq_rows, coeff, table, previous):
    model_width = momentum.shape[1]
    block_cols = momentum.shape[2] // freq_rows.shape[0]
    freqs = freq_rows.shape[2]
    half = model_width // 2
    tile = min(512, half)
    steps = half // tile

    def kernel(freq, mom_a, mom_b, grad_a, grad_b, coeff_ref, table_ref, *rest):
        residual, both, buffer, sems = rest[-4:]
        step = pl.program_id(0)
        slot = step % 2

        def copies(at, where):
            lanes = pl.ds(column_block * block_cols, block_cols)
            return [
                pltpu.make_async_copy(
                    buffer.at[where, k], residual.at[0, pl.ds(start * tile, tile), lanes],
                    sems.at[where, k],
                )
                for k, start in enumerate((at, 2 * steps - 1 - at))
            ]

        @pl.when(step == 0)
        def _():
            both[:block_cols] = coeff_ref[...]
            both[block_cols:] = (coeff_ref[...].astype(f32) * parity_sign(freq[0])).astype(bf16)

        back = dot_nt(table_ref[...], both[...])

        @pl.when(step >= 2)
        def _():
            for copy in copies(step - 2, slot):
                copy.wait()

        buffer[slot, 0] = (
            momentum_decay * mom_a[0] + grad_a[0].astype(f32) - back[:, :block_cols]
        )
        buffer[slot, 1] = (
            momentum_decay * mom_b[0] + grad_b[0].astype(f32) - flip_wide(back[:, block_cols:])
        )
        for copy in copies(step, slot):
            copy.start()

        @pl.when(step == steps - 1)
        def _():
            if steps > 1:
                for copy in copies(step - 1, 1 - slot):
                    copy.wait()
            for copy in copies(step, slot):
                copy.wait()

    def rows(which):
        def index(step):
            return (0, 2 * steps - 1 - step if which else step, column_block)

        return pl.BlockSpec((1, tile, block_cols), index)

    operands = [freq_rows, momentum, momentum, gradient, gradient, coeff, table]
    specs = [
        pl.BlockSpec((1, 1, freqs), lambda step: (column_block, 0, 0)),
        rows(0), rows(1), rows(0), rows(1),
        pl.BlockSpec((block_cols, freqs), lambda step: (0, 0)),
        pl.BlockSpec((tile, freqs), lambda step: (step, 0)),
    ]
    aliases = {}
    if previous is not None:
        aliases = {len(operands): 0}
        operands.append(previous)
        specs.append(pl.BlockSpec(memory_space=pl.ANY))
    return pl.pallas_call(
        kernel,
        name=f"remain_{column_block}",
        grid=(steps,),
        in_specs=specs,
        out_specs=pl.BlockSpec(memory_space=pl.ANY),
        scratch_shapes=[
            pltpu.VMEM((2 * block_cols, freqs), bf16),
            pltpu.VMEM((2, 2, tile, block_cols), f32),
            pltpu.SemaphoreType.DMA((2, 2)),
        ],
        out_shape=jax.ShapeDtypeStruct(momentum.shape, f32),
        input_output_aliases=aliases,
    )(*operands)


def spread(tokens, meta, dp, tensor):
    token_rows, width = tokens.shape
    ratio = dp // tensor
    rows, lanes = token_rows // tensor, width // ratio

    def kernel(meta_ref, tokens_ref, *outs):
        for k in range(dp):
            part = meta_ref[0] ^ k
            outs[k][...] = tokens_ref[
                pl.ds(pl.multiple_of((part % tensor) * rows, rows), rows),
                pl.ds(pl.multiple_of((part // tensor) * lanes, lanes), lanes),
            ]

    return pl.pallas_call(
        kernel,
        name="spread",
        in_specs=[pl.BlockSpec(memory_space=pltpu.SMEM), pl.BlockSpec(memory_space=pltpu.VMEM)],
        out_specs=[pl.BlockSpec(memory_space=pltpu.VMEM)] * dp,
        out_shape=[jax.ShapeDtypeStruct((rows, lanes), bf16)] * dp,
    )(meta, tokens)


def apply(masters, freq_rows, means, feature_parts, meta, model_width, dp, tensor, group):
    own_rows, cols = masters.shape
    blocks, _, freqs = freq_rows.shape
    block_cols = cols // blocks
    piece = block_cols // group
    _, part_rows, part_lanes = feature_parts[0].shape
    token_rows = part_rows * tensor
    ratio = dp // tensor

    def kernel(meta_ref, freq, masters_ref, *rest):
        mean_refs = rest[: blocks * group]
        feature_refs = rest[blocks * group : blocks * group + tensor]
        rest = rest[blocks * group + tensor :]
        new_ref, outs = rest[0], rest[1 : 1 + dp]
        table, mean, weights, coarse_cos, coarse_sin, fine_cos, fine_sin = rest[1 + dp :]
        device, rank = meta_ref[0], meta_ref[1]
        for block in range(blocks):
            fill_tables(
                freq[block], device * own_rows, coarse_cos, coarse_sin, fine_cos, fine_sin,
                model_width,
            )
            fill_cosines(
                table, 0, own_rows // fine_rows, coarse_cos, coarse_sin, fine_cos, fine_sin
            )
            for k in range(group):
                start = ((device % group) ^ k) * piece
                mean[pl.ds(pl.multiple_of(start, piece), piece), :] = mean_refs[
                    block * group + k
                ][...]
            update = dot_nt(table[...], mean[...]) * (1.0 / dp)
            lanes = pl.ds(block * block_cols, block_cols)
            fresh = masters_ref[:, lanes] - step_rate * update
            new_ref[:, lanes] = fresh
            weights[:, lanes] = fresh.astype(bf16)
        for k in range(dp):
            target = device ^ k
            gathered = []
            for other in range(tensor):
                holder = rank ^ other
                message = target ^ ((device % ratio) * tensor + holder)
                gathered.append(feature_refs[other][message])
            products = jnp.dot(
                jnp.concatenate(gathered, axis=0), weights[...], preferred_element_type=f32
            )
            for other in range(tensor):
                start = (rank ^ other) * part_rows
                outs[k][pl.ds(pl.multiple_of(start, part_rows), part_rows), :] = products[
                    other * part_rows : (other + 1) * part_rows
                ].astype(bf16)

    vmem = pl.BlockSpec(memory_space=pltpu.VMEM)
    return pl.pallas_call(
        kernel,
        name="apply",
        in_specs=[pl.BlockSpec(memory_space=pltpu.SMEM)]
        + [vmem] * (2 + blocks * group + tensor),
        out_specs=[vmem] * (1 + dp),
        out_shape=[jax.ShapeDtypeStruct((own_rows, cols), f32)]
        + [jax.ShapeDtypeStruct((token_rows, cols), bf16)] * dp,
        scratch_shapes=[
            pltpu.VMEM((own_rows, freqs), bf16),
            pltpu.VMEM((block_cols, freqs), bf16),
            pltpu.VMEM((own_rows, cols), bf16),
        ]
        + [pltpu.VMEM((own_rows // fine_rows, freqs), f32)] * 2
        + [pltpu.VMEM((fine_rows, freqs), f32)] * 2,
    )(meta, freq_rows, masters, *means, *feature_parts)


def swap(value, axis, mask, size):
    return lax.ppermute(value, axis, [(k, k ^ mask) for k in range(size)])


def sum_low(values):
    total = values[0].astype(f32)
    for value in values[1:]:
        total = total + value.astype(f32)
    return total.astype(bf16)


def body(momentum, gradient, masters, tokens, freq_index):
    dp, tensor = lax.axis_size("dp"), lax.axis_size("tensor")
    group = min(4, dp)
    ratio = dp // tensor
    blocks = freq_index.shape[0]
    model_width = momentum.shape[1]
    device, rank = lax.axis_index("dp"), lax.axis_index("tensor")
    meta = jnp.stack([device, rank]).astype(jnp.int32)
    freq_rows = freq_index[:, None, :]

    sent = spread(tokens, meta, dp, tensor)
    received = []
    for k in range(dp):
        pairs = []
        for source in range(dp):
            for holder in range(tensor):
                part = source ^ k
                target = (holder * ratio + part // tensor) * tensor + part % tensor
                pairs.append((source * tensor + holder, target))
        received.append(lax.ppermute(sent[k], ("dp", "tensor"), pairs))
    features = {0: jnp.stack(received)}
    mask = tensor // 2
    while mask > 0:
        for held in sorted(features):
            features[held ^ mask] = swap(features[held], "tensor", mask, tensor)
        mask //= 2
    feature_parts = [features[k] for k in range(tensor)]

    residual = None
    means = []
    forwards = [
        forward(block, momentum, gradient, freq_rows, meta, group) for block in range(blocks)
    ]
    for block in range(blocks):
        pieces = forwards[block][1 : 1 + group]
        summed = sum_low(
            [pieces[0]] + [swap(pieces[k], "dp", k, dp) for k in range(1, group)]
        )
        summed = sum_low(
            [summed] + [swap(summed, "dp", k * group, dp) for k in range(1, dp // group)]
        )
        means += [summed] + [swap(summed, "dp", k, dp) for k in range(1, group)]
    for block in range(blocks):
        residual = remain(
            block, momentum, gradient, freq_rows, forwards[block][0], forwards[block][-1], residual
        )
    new_masters, *partials = apply(
        masters, freq_rows, means, feature_parts, meta, model_width, dp, tensor, group
    )
    total = partials[0].astype(f32)
    for k in range(1, dp):
        total = total + swap(partials[k], "dp", k, dp).astype(f32)
    projected = (total * model_width ** (-0.5)).astype(bf16)
    return (residual, new_masters, projected)


def solution(mesh):
    return jax.shard_map(
        body,
        mesh=mesh,
        in_specs=(
            P("dp", None, "tensor"),
            P("dp", None, "tensor"),
            P("dp", "tensor"),
            P("dp", "tensor"),
            P("tensor", None),
        ),
        out_specs=(P("dp", None, "tensor"), P("dp", "tensor"), P("dp", "tensor")),
        check_vma=False,
    )
```

```python
import math

import jax
import jax.numpy as jnp
from jax import lax
from jax.experimental import pallas as pl
from jax.experimental.pallas import tpu as pltpu
from jax.sharding import PartitionSpec as P


momentum_decay = 0.9
step_rate = 1.0
fine_rows = 64
forward_tile = 1024
flip_rows = 128
f32 = jnp.float32
bf16 = jnp.bfloat16


def wrap(phase, period):
    return phase & (period - 1) if period & (period - 1) == 0 else phase % period


def sine_cosine(phase, model_width):
    shifted = phase + model_width // 2
    if model_width & (model_width - 1) == 0:
        quarter = shifted >> (model_width.bit_length() - 1)
    else:
        quarter = shifted // model_width
    x = (phase - quarter * model_width).astype(f32) * (math.pi / (2 * model_width))
    z = x * x
    sine = x + x * z * (-1.6666654611e-1 + z * (8.3321608736e-3 + z * -1.9515295891e-4))
    cosine = 1.0 - 0.5 * z + z * z * (
        4.166664568298827e-2 + z * (-1.388731625493765e-3 + z * 2.443315711809948e-5)
    )
    swapped = (quarter & 1) == 1
    cos_sign = (1 - ((quarter + 1) & 2)).astype(f32)
    sin_sign = (1 - (quarter & 2)).astype(f32)
    return (
        cos_sign * jnp.where(swapped, sine, cosine),
        sin_sign * jnp.where(swapped, cosine, sine),
    )


def fill_tables(frequency, coarse_cos, coarse_sin, fine_cos, fine_sin, model_width):
    freqs = frequency.shape[1]
    digit = lax.broadcasted_iota(jnp.int32, (8, freqs), 0)
    scale = jnp.where(
        frequency == 0, math.sqrt(1.0 / model_width), math.sqrt(2.0 / model_width)
    ).astype(f32)

    def angles(multiplier):
        return sine_cosine(wrap(multiplier * frequency, 4 * model_width), model_width)

    def combine(high, low, cos_ref, sin_ref):
        for k in range(cos_ref.shape[0] // 8):
            rows = pl.ds(8 * k, 8)
            cosine, sine = high[0][k : k + 1], high[1][k : k + 1]
            cos_ref[rows, :] = cosine * low[0] - sine * low[1]
            sin_ref[rows, :] = sine * low[0] + cosine * low[1]

    cosine, sine = angles(2 * fine_rows * digit)
    combine(
        angles(16 * fine_rows * digit), (cosine * scale, sine * scale), coarse_cos, coarse_sin
    )
    combine(angles(16 * digit), angles(2 * digit + 1), fine_cos, fine_sin)


def fill_cosines(target, first_coarse, count, coarse_cos, coarse_sin, fine_cos, fine_sin):
    for lane in range(0, target.shape[1], 128):
        lanes = pl.ds(lane, 128)
        cosine = fine_cos[:, lanes]
        sine = fine_sin[:, lanes]
        coarse_c = coarse_cos[pl.ds(first_coarse, count), lanes]
        coarse_s = coarse_sin[pl.ds(first_coarse, count), lanes]
        for k in range(count):
            target[pl.ds(k * fine_rows, fine_rows), lanes] = (
                coarse_c[k : k + 1] * cosine - coarse_s[k : k + 1] * sine
            ).astype(bf16)


def reversal():
    rows = lax.broadcasted_iota(jnp.int32, (flip_rows, flip_rows), 0)
    cols = lax.broadcasted_iota(jnp.int32, (flip_rows, flip_rows), 1)
    return jnp.where(rows + cols == flip_rows - 1, 1.0, 0.0).astype(bf16)


def flip_low(value):
    flips = reversal()
    pieces = [
        jnp.dot(flips, value[lower : lower + flip_rows], preferred_element_type=f32)
        for lower in range(value.shape[0] - flip_rows, -1, -flip_rows)
    ]
    return jnp.concatenate(pieces, axis=0)


def flip_wide(value):
    high = value.astype(bf16)
    low = (value - high.astype(f32)).astype(bf16)
    return flip_low(high) + flip_low(low)


def parity_sign(frequency):
    return (1 - 2 * (frequency & 1)).astype(f32)


def dot_tn(a, b):
    return lax.dot_general(a, b, (((0,), (0,)), ((), ())), preferred_element_type=f32)


def dot_nt(a, b):
    return lax.dot_general(a, b, (((1,), (1,)), ((), ())), preferred_element_type=f32)


def forward(momentum, gradient, freq_rows, meta, group):
    model_width = momentum.shape[1]
    blocks, _, freqs = freq_rows.shape
    cols = momentum.shape[2]
    block_cols = cols // blocks
    half = model_width // 2
    tile = min(forward_tile, half)
    steps = half // tile
    piece = cols // group

    def kernel(meta_ref, freq, mom_a, mom_b, grad_a, grad_b, coeff, *rest):
        pieces = rest[:group]
        table, total, coarse_cos, coarse_sin, fine_cos, fine_sin = rest[group:]
        block, step = pl.program_id(0), pl.program_id(1)
        frequency = freq[0]

        @pl.when(step == 0)
        def _():
            fill_tables(frequency, coarse_cos, coarse_sin, fine_cos, fine_sin, model_width)

        fill_cosines(
            table, pl.multiple_of(step * (tile // fine_rows), tile // fine_rows),
            tile // fine_rows, coarse_cos, coarse_sin, fine_cos, fine_sin,
        )
        low_a = (momentum_decay * mom_a[0] + grad_a[0].astype(f32)).astype(bf16)
        low_b = (momentum_decay * mom_b[0] + grad_b[0].astype(f32)).astype(bf16)
        both = jnp.concatenate([low_a, flip_low(low_b).astype(bf16)], axis=1)
        partial = dot_tn(both, table[...])

        @pl.when(step == 0)
        def _():
            total[...] = partial

        @pl.when(step > 0)
        def _():
            total[...] += partial

        @pl.when(step == steps - 1)
        def _():
            rows = pl.ds(pl.multiple_of(block * block_cols, block_cols), block_cols)
            coeff[rows, :] = (
                total[:block_cols] + parity_sign(frequency) * total[block_cols:]
            ).astype(bf16)

        @pl.when((step == steps - 1) & (block == blocks - 1))
        def _():
            for k in range(group):
                start = ((meta_ref[0] % group) ^ k) * piece
                pieces[k][...] = coeff[pl.ds(pl.multiple_of(start, piece), piece), :]

    def rows(which):
        def index(block, step, meta_ref):
            return (0, 2 * steps - 1 - step if which else step, block)

        return pl.BlockSpec((1, tile, block_cols), index)

    whole = lambda block, step, meta_ref: (0, 0)
    return pl.pallas_call(
        kernel,
        name="forward",
        grid_spec=pltpu.PrefetchScalarGridSpec(
            num_scalar_prefetch=1,
            grid=(blocks, steps),
            in_specs=[
                pl.BlockSpec((1, 1, freqs), lambda block, step, meta_ref: (block, 0, 0)),
                rows(0), rows(1), rows(0), rows(1),
            ],
            out_specs=[pl.BlockSpec((cols, freqs), whole)]
            + [pl.BlockSpec((piece, freqs), whole)] * group
            + [pl.BlockSpec(
                (tile, freqs), lambda block, step, meta_ref: (block * steps + step, 0)
            )],
            scratch_shapes=[pltpu.VMEM((2 * block_cols, freqs), f32)]
            + [pltpu.VMEM((half // fine_rows, freqs), f32)] * 2
            + [pltpu.VMEM((fine_rows, freqs), f32)] * 2,
        ),
        out_shape=[jax.ShapeDtypeStruct((cols, freqs), bf16)]
        + [jax.ShapeDtypeStruct((piece, freqs), bf16)] * group
        + [jax.ShapeDtypeStruct((blocks * half, freqs), bf16)],
    )(meta, freq_rows, momentum, momentum, gradient, gradient)


def remain(part, parts, momentum, gradient, freq_rows, coeff, table, previous):
    model_width = momentum.shape[1]
    block_cols = momentum.shape[2] // freq_rows.shape[0]
    freqs = freq_rows.shape[2]
    half = model_width // 2
    tile = min(512, half)
    all_steps = half // tile
    blocks = freq_rows.shape[0]
    column_block = part * blocks // parts
    steps = all_steps * blocks // parts
    first = part * steps - column_block * all_steps

    def kernel(freq, mom_a, mom_b, grad_a, grad_b, coeff_ref, table_ref, *rest):
        residual, both, buffer, sems = rest[-4:]
        step = pl.program_id(0)
        slot = step % 2

        def copies(at, where):
            lanes = pl.ds(column_block * block_cols, block_cols)
            return [
                pltpu.make_async_copy(
                    buffer.at[where, k], residual.at[0, pl.ds(start * tile, tile), lanes],
                    sems.at[where, k],
                )
                for k, start in enumerate((first + at, 2 * all_steps - 1 - first - at))
            ]

        @pl.when(step == 0)
        def _():
            both[:block_cols] = coeff_ref[...]
            both[block_cols:] = (coeff_ref[...].astype(f32) * parity_sign(freq[0])).astype(bf16)

        back = dot_nt(table_ref[...], both[...])

        @pl.when(step >= 2)
        def _():
            for copy in copies(step - 2, slot):
                copy.wait()

        buffer[slot, 0] = (
            momentum_decay * mom_a[0] + grad_a[0].astype(f32) - back[:, :block_cols]
        )
        buffer[slot, 1] = (
            momentum_decay * mom_b[0] + grad_b[0].astype(f32) - flip_wide(back[:, block_cols:])
        )
        for copy in copies(step, slot):
            copy.start()

        @pl.when(step == steps - 1)
        def _():
            if steps > 1:
                for copy in copies(step - 1, 1 - slot):
                    copy.wait()
            for copy in copies(step, slot):
                copy.wait()

    def rows(which):
        def index(step):
            at = first + step
            return (0, 2 * all_steps - 1 - at if which else at, column_block)

        return pl.BlockSpec((1, tile, block_cols), index)

    operands = [freq_rows, momentum, momentum, gradient, gradient, coeff, table]
    specs = [
        pl.BlockSpec((1, 1, freqs), lambda step: (column_block, 0, 0)),
        rows(0), rows(1), rows(0), rows(1),
        pl.BlockSpec((block_cols, freqs), lambda step: (column_block, 0)),
        pl.BlockSpec(
            (tile, freqs), lambda step: (column_block * all_steps + first + step, 0)
        ),
    ]
    aliases = {}
    if previous is not None:
        aliases = {len(operands): 0}
        operands.append(previous)
        specs.append(pl.BlockSpec(memory_space=pl.ANY))
    return pl.pallas_call(
        kernel,
        grid=(steps,),
        in_specs=specs,
        out_specs=pl.BlockSpec(memory_space=pl.ANY),
        scratch_shapes=[
            pltpu.VMEM((2 * block_cols, freqs), bf16),
            pltpu.VMEM((2, 2, tile, block_cols), f32),
            pltpu.SemaphoreType.DMA((2, 2)),
        ],
        out_shape=jax.ShapeDtypeStruct(momentum.shape, f32),
        input_output_aliases=aliases,
    )(*operands)


def apply(masters, freq_rows, table, means, features, meta, dp, tensor, group):
    own_rows, cols = masters.shape
    blocks, _, freqs = freq_rows.shape
    block_cols = cols // blocks
    piece = cols // group
    ratio, token_rows, _ = features[0].shape
    half_parts = table.shape[0] // blocks // own_rows
    crosses = dp // group

    def kernel(meta_ref, freq, masters_ref, *rest):
        tables = rest[:blocks]
        mean_refs = rest[blocks : blocks + group]
        feature_refs = rest[blocks + group : blocks + group + tensor]
        new_ref, *outs, mean, weights, products = rest[blocks + group + tensor :]
        device, rank = meta_ref[0], meta_ref[1]
        mirrored = device >= half_parts
        for k in range(group):
            start = ((device % group) ^ k) * piece
            mean[pl.ds(pl.multiple_of(start, piece), piece), :] = mean_refs[k][...]
        for block in range(blocks):
            sign = jnp.where(mirrored, parity_sign(freq[block]), 1.0)
            lanes = pl.ds(block * block_cols, block_cols)
            own = (mean[lanes, :].astype(f32) * sign).astype(bf16)
            update = dot_nt(tables[block][...], own) * (1.0 / dp)

            @pl.when(mirrored)
            def _():
                new_ref[:, lanes] = masters_ref[:, lanes] - step_rate * flip_wide(update)

            @pl.when(jnp.logical_not(mirrored))
            def _():
                new_ref[:, lanes] = masters_ref[:, lanes] - step_rate * update

        weights[...] = new_ref[...].astype(bf16)
        for other in range(tensor):
            for k in range(ratio):
                target = (rank ^ other) * ratio + ((device % ratio) ^ k)
                products[target ^ device] = jnp.dot(
                    feature_refs[other][k], weights[...], preferred_element_type=f32
                ).astype(bf16)
        for k in range(group):
            for cross in range(crosses):
                outs[k][cross] = products[cross * group + k]

    def whole(*shape):
        return pl.BlockSpec(shape, lambda step, meta_ref: (0,) * len(shape))

    def own_table(block):
        def index(step, meta_ref):
            device = meta_ref[0]
            row = jnp.where(device >= half_parts, 2 * half_parts - 1 - device, device)
            return (block * half_parts + row, 0)

        return pl.BlockSpec((own_rows, freqs), index)

    return pl.pallas_call(
        kernel,
        name="apply",
        grid_spec=pltpu.PrefetchScalarGridSpec(
            num_scalar_prefetch=1,
            grid=(1,),
            in_specs=[whole(*freq_rows.shape), whole(own_rows, cols)]
            + [own_table(block) for block in range(blocks)]
            + [whole(piece, freqs)] * group
            + [whole(*features[0].shape)] * tensor,
            out_specs=[whole(own_rows, cols)] + [whole(crosses, token_rows, cols)] * group,
            scratch_shapes=[
                pltpu.VMEM((cols, freqs), bf16),
                pltpu.VMEM((own_rows, cols), bf16),
                pltpu.VMEM((dp, token_rows, cols), bf16),
            ],
        ),
        out_shape=[jax.ShapeDtypeStruct((own_rows, cols), f32)]
        + [jax.ShapeDtypeStruct((crosses, token_rows, cols), bf16)] * group,
    )(meta, freq_rows, masters, *[table] * blocks, *means, *features)


def swap(value, axis, mask, size):
    return lax.ppermute(value, axis, [(k, k ^ mask) for k in range(size)])


def sum_low(values):
    total = values[0].astype(f32)
    for value in values[1:]:
        total = total + value.astype(f32)
    return total.astype(bf16)


def step(momentum, gradient, masters, tokens, freq_index):
    dp, tensor = lax.axis_size("dp"), lax.axis_size("tensor")
    group = min(4, dp)
    ratio = dp // tensor
    model_width = momentum.shape[1]
    device, rank = lax.axis_index("dp"), lax.axis_index("tensor")
    meta = jnp.stack([device, rank]).astype(jnp.int32)
    freq_rows = freq_index[:, None, :]

    pairs = [
        ((J * ratio + h) * tensor + j, (j * ratio + h) * tensor + J)
        for J in range(tensor) for h in range(ratio) for j in range(tensor)
    ]
    traded = lax.ppermute(tokens, ("dp", "tensor"), pairs)
    width = tokens.shape[1] // ratio

    coeff, *pieces, table = forward(momentum, gradient, freq_rows, meta, group)

    def feature_piece(k):
        start = ((device % ratio) ^ k) * width
        return lax.dynamic_slice_in_dim(traded, start, width, axis=1)

    parts = [feature_piece(0)]
    for k in range(1, ratio):
        parts.append(swap(feature_piece(k), "dp", k, dp))
    first = [swap(pieces[k], "dp", k, dp) for k in range(1, group)]

    residual = None
    remain_parts = 4

    def next_remain(part, residual):
        return remain(
            part, remain_parts, momentum, gradient, freq_rows, coeff, table, residual
        )

    residual = next_remain(0, residual)
    features = {0: jnp.stack(parts)}
    mask = tensor // 2
    while mask > 0:
        for held in sorted(features):
            features[held ^ mask] = swap(features[held], "tensor", mask, tensor)
        mask //= 2
    summed = sum_low([pieces[0]] + first)
    summed = sum_low([summed] + [swap(summed, "dp", k * group, dp) for k in range(1, dp // group)])
    residual = next_remain(1, residual)
    means = [summed] + [swap(summed, "dp", k, dp) for k in range(1, group)]
    residual = next_remain(2, residual)
    new_masters, *partials = apply(
        masters, freq_rows, table, means, [features[k] for k in range(tensor)], meta, dp, tensor,
        group,
    )
    received = [swap(partials[k], "dp", k, dp) for k in range(1, group)]
    residual = next_remain(3, residual)
    part = partials[0].astype(f32)
    for value in received:
        part = part + value.astype(f32)
    part_low = part.astype(bf16)
    total = part[0]
    for k in range(1, dp // group):
        total = total + swap(part_low[k], "dp", k * group, dp).astype(f32)
    projected = (total * model_width ** (-0.5)).astype(bf16)
    return (residual, new_masters, projected)


def solution(mesh):
    return jax.shard_map(
        step,
        mesh=mesh,
        in_specs=(
            P("dp", None, "tensor"),
            P("dp", None, "tensor"),
            P("dp", "tensor"),
            P("dp", "tensor"),
            P("tensor", None),
        ),
        out_specs=(P("dp", None, "tensor"), P("dp", "tensor"), P("dp", "tensor")),
        check_vma=False,
    )
```

```python
import math

import jax
import jax.numpy as jnp
from jax import lax
from jax.experimental import pallas as pl
from jax.experimental.pallas import tpu as pltpu
from jax.sharding import PartitionSpec as P


momentum_decay = 0.9
step_rate = 1.0
fine_rows = 64
forward_tile = 1024
remain_shares = (0, 4, 8, 12, 13, 15, 16)
apply_rows = 1024
vmem_bytes = 40 * 1024 * 1024
f32 = jnp.float32
bf16 = jnp.bfloat16


def wrap(phase, period):
    return phase & (period - 1) if period & (period - 1) == 0 else phase % period


def sine_cosine(phase, model_width):
    shifted = phase + model_width // 2
    if model_width & (model_width - 1) == 0:
        quarter = shifted >> (model_width.bit_length() - 1)
    else:
        quarter = shifted // model_width
    x = (phase - quarter * model_width).astype(f32) * (math.pi / (2 * model_width))
    z = x * x
    sine = x + x * z * (-1.6666654611e-1 + z * (8.3321608736e-3 + z * -1.9515295891e-4))
    cosine = 1.0 - 0.5 * z + z * z * (
        4.166664568298827e-2 + z * (-1.388731625493765e-3 + z * 2.443315711809948e-5)
    )
    swapped = (quarter & 1) == 1
    cos_sign = (1 - ((quarter + 1) & 2)).astype(f32)
    sin_sign = (1 - (quarter & 2)).astype(f32)
    return (
        cos_sign * jnp.where(swapped, sine, cosine),
        sin_sign * jnp.where(swapped, cosine, sine),
    )


def fill_tables(frequency, coarse_cos, coarse_sin, fine_cos, fine_sin, twice, model_width):
    freqs = frequency.shape[1]
    digit = lax.broadcasted_iota(jnp.int32, (8, freqs), 0)
    scale = jnp.where(
        frequency == 0, math.sqrt(1.0 / model_width), math.sqrt(2.0 / model_width)
    ).astype(f32)

    def angles(multiplier):
        return sine_cosine(wrap(multiplier * frequency, 4 * model_width), model_width)

    def combine(high, low, cos_ref, sin_ref):
        for k in range(cos_ref.shape[0] // 8):
            rows = pl.ds(8 * k, 8)
            cosine, sine = high[0][k : k + 1], high[1][k : k + 1]
            cos_ref[rows, :] = cosine * low[0] - sine * low[1]
            sin_ref[rows, :] = sine * low[0] + cosine * low[1]

    cosine, sine = angles(2 * fine_rows * digit)
    twice[...] = 2.0 * jnp.broadcast_to(cosine[1:2], cosine.shape)
    combine(
        angles(16 * fine_rows * digit), (cosine * scale, sine * scale), coarse_cos, coarse_sin
    )
    combine(angles(16 * digit), angles(2 * digit + 1), fine_cos, fine_sin)


def fill_cosines(target, first_coarse, count, coarse_cos, coarse_sin, fine_cos, fine_sin, twice):
    for lane in range(0, target.shape[1], 128):
        lanes = pl.ds(lane, 128)
        cosine = fine_cos[:, lanes]
        sine = fine_sin[:, lanes]
        coarse_c = coarse_cos[pl.ds(first_coarse, 8), lanes]
        coarse_s = coarse_sin[pl.ds(first_coarse, 8), lanes]
        factor = jnp.broadcast_to(twice[0:1, lanes], cosine.shape)
        older = newer = None
        for k in range(count):
            if k < 2:
                value = coarse_c[k : k + 1] * cosine - coarse_s[k : k + 1] * sine
            else:
                value = factor * newer - older
            older, newer = newer, value
            target[pl.ds(k * fine_rows, fine_rows), lanes] = value.astype(bf16)


def flip(value):
    order = 7 - lax.broadcasted_iota(jnp.int32, (8, value.shape[1]), 0)
    pieces = [
        jnp.take_along_axis(value[row : row + 8], order, axis=0)
        for row in range(value.shape[0] - 8, -1, -8)
    ]
    return jnp.concatenate(pieces, axis=0)


def parity_sign(frequency):
    return (1 - 2 * (frequency & 1)).astype(f32)


def dot_tn(a, b):
    return lax.dot_general(a, b, (((0,), (0,)), ((), ())), preferred_element_type=f32)


def dot_nt(a, b):
    return lax.dot_general(a, b, (((1,), (1,)), ((), ())), preferred_element_type=f32)


def forward(momentum, gradient, freq_rows, meta, group):
    model_width = momentum.shape[1]
    blocks, freqs = freq_rows.shape
    cols = momentum.shape[2]
    block_cols = cols // blocks
    half = model_width // 2
    tile = min(forward_tile, half)
    steps = half // tile
    piece = cols // group

    def kernel(device_ref, rank_ref, freq, mom_a, mom_b, grad_a, grad_b, coeff, *rest):
        pieces = rest[:group]
        table, total, *tables = rest[group:]
        block, step = pl.program_id(0), pl.program_id(1)
        frequency = freq[0:1]
        for other in range(1, blocks):
            frequency = jnp.where(block == other, freq[other : other + 1], frequency)

        @pl.when(step == 0)
        def _():
            fill_tables(frequency, *tables, model_width)

        fill_cosines(
            table, pl.multiple_of(step * (tile // fine_rows), 8), tile // fine_rows, *tables
        )
        low_a = (momentum_decay * mom_a[0] + grad_a[0].astype(f32)).astype(bf16)
        low_b = flip(momentum_decay * mom_b[0] + grad_b[0].astype(f32)).astype(bf16)
        both = jnp.concatenate([low_a, low_b], axis=1)
        partial = dot_tn(both, table[...])

        @pl.when(step == 0)
        def _():
            total[...] = partial

        @pl.when(step > 0)
        def _():
            total[...] += partial

        @pl.when(step == steps - 1)
        def _():
            rows = pl.ds(pl.multiple_of(block * block_cols, block_cols), block_cols)
            coeff[rows, :] = (
                total[:block_cols] + parity_sign(frequency) * total[block_cols:]
            ).astype(bf16)

        @pl.when((step == steps - 1) & (block == blocks - 1))
        def _():
            for k in range(group):
                start = ((device_ref[0] % group) ^ k) * piece
                pieces[k][...] = coeff[pl.ds(pl.multiple_of(start, piece), piece), :]

    def whole(block, step, *scalars):
        return (0, 0)

    def rows(which):
        def index(block, step, *scalars):
            return (0, 2 * steps - 1 - step if which else step, block)

        return pl.BlockSpec((1, tile, block_cols), index)

    return pl.pallas_call(
        kernel,
        name="forward",
        grid_spec=pltpu.PrefetchScalarGridSpec(
            num_scalar_prefetch=2,
            grid=(blocks, steps),
            in_specs=[
                pl.BlockSpec((blocks, freqs), whole),
                rows(0), rows(1), rows(0), rows(1),
            ],
            out_specs=[pl.BlockSpec((cols, freqs), whole)]
            + [pl.BlockSpec((piece, freqs), whole)] * group
            + [pl.BlockSpec(
                (tile, freqs), lambda block, step, *scalars: (block * steps + step, 0)
            )],
            scratch_shapes=[pltpu.VMEM((2 * block_cols, freqs), f32)]
            + [pltpu.VMEM((half // fine_rows, freqs), f32)] * 2
            + [pltpu.VMEM((fine_rows, freqs), f32)] * 2
            + [pltpu.VMEM((8, freqs), f32)],
        ),
        out_shape=[jax.ShapeDtypeStruct((cols, freqs), bf16)]
        + [jax.ShapeDtypeStruct((piece, freqs), bf16)] * group
        + [jax.ShapeDtypeStruct((blocks * half, freqs), bf16)],
    )(*meta, freq_rows, momentum, momentum, gradient, gradient)


def remain(part, momentum, gradient, freq_rows, coeff, table, previous):
    model_width = momentum.shape[1]
    block_cols = momentum.shape[2] // freq_rows.shape[0]
    blocks, freqs = freq_rows.shape
    half = model_width // 2
    tile = min(512 if blocks > 1 else 256, half)
    all_steps = half // tile
    begin, end = (all_steps * blocks * share // 16 for share in remain_shares[part : part + 2])
    column_block, first = divmod(begin, all_steps)
    steps = end - begin

    def kernel(freq, mom_a, mom_b, grad_a, grad_b, coeff_ref, table_ref, *rest):
        residual, both, buffer, sems = rest[-4:]
        step = pl.program_id(0)
        slot = step % 2

        def copies(at, where):
            lanes = pl.ds(column_block * block_cols, block_cols)
            return [
                pltpu.make_async_copy(
                    buffer.at[where, k], residual.at[0, pl.ds(start * tile, tile), lanes],
                    sems.at[where, k],
                )
                for k, start in enumerate((first + at, 2 * all_steps - 1 - first - at))
            ]

        @pl.when(step == 0)
        def _():
            both[:block_cols] = coeff_ref[...]
            both[block_cols:] = (coeff_ref[...].astype(f32) * parity_sign(freq[column_block : column_block + 1])).astype(bf16)

        back = dot_nt(table_ref[...], both[...])

        @pl.when(step >= 2)
        def _():
            for copy in copies(step - 2, slot):
                copy.wait()

        buffer[slot, 0] = (
            momentum_decay * mom_a[0] + grad_a[0].astype(f32) - back[:, :block_cols]
        )
        buffer[slot, 1] = (
            momentum_decay * mom_b[0] + grad_b[0].astype(f32) - flip(back[:, block_cols:])
        )
        for copy in copies(step, slot):
            copy.start()

        @pl.when(step == steps - 1)
        def _():
            if steps > 1:
                for copy in copies(step - 1, 1 - slot):
                    copy.wait()
            for copy in copies(step, slot):
                copy.wait()

    def rows(which):
        def index(step):
            at = first + step
            return (0, 2 * all_steps - 1 - at if which else at, column_block)

        return pl.BlockSpec((1, tile, block_cols), index)

    operands = [freq_rows, momentum, momentum, gradient, gradient, coeff, table]
    specs = [
        pl.BlockSpec((blocks, freqs), lambda step: (0, 0)),
        rows(0), rows(1), rows(0), rows(1),
        pl.BlockSpec((block_cols, freqs), lambda step: (column_block, 0)),
        pl.BlockSpec(
            (tile, freqs), lambda step: (column_block * all_steps + first + step, 0)
        ),
    ]
    aliases = {}
    if previous is not None:
        aliases = {len(operands): 0}
        operands.append(previous)
        specs.append(pl.BlockSpec(memory_space=pl.ANY))
    return pl.pallas_call(
        kernel,
        grid=(steps,),
        in_specs=specs,
        out_specs=pl.BlockSpec(memory_space=pl.ANY),
        scratch_shapes=[
            pltpu.VMEM((2 * block_cols, freqs), bf16),
            pltpu.VMEM((2, 2, tile, block_cols), f32),
            pltpu.SemaphoreType.DMA((2, 2)),
        ],
        out_shape=jax.ShapeDtypeStruct(momentum.shape, f32),
        input_output_aliases=aliases,
    )(*operands)


def apply(masters, freq_rows, table, means, features, meta, dp, tensor, group):
    own_rows, cols = masters.shape
    blocks, freqs = freq_rows.shape
    block_cols = cols // blocks
    piece = cols // group
    ratio, token_rows, _ = features[0].shape
    half_parts = table.shape[0] // blocks // own_rows
    crosses = dp // group

    chunk = min(apply_rows, own_rows)
    steps = own_rows // chunk

    def kernel(device_ref, rank_ref, freq, masters_ref, *rest):
        tables = rest[:blocks]
        mean_refs = rest[blocks : blocks + group]
        feature_refs = rest[blocks + group : blocks + group + tensor]
        new_ref, *outs, mean, products = rest[blocks + group + tensor :]
        device, rank = device_ref[0], rank_ref[0]
        step = pl.program_id(0)
        mirrored = device >= half_parts

        @pl.when(step == 0)
        def _():
            for k in range(group):
                start = ((device % group) ^ k) * piece
                mean[pl.ds(pl.multiple_of(start, piece), piece), :] = mean_refs[k][...]
            for block in range(blocks):
                rows = pl.ds(block * block_cols, block_cols)
                sign = jnp.where(mirrored, parity_sign(freq[block : block + 1]), 1.0)
                mean[rows, :] = (mean[rows, :].astype(f32) * sign).astype(bf16)

        updates = [
            dot_nt(tables[block][...], mean[pl.ds(block * block_cols, block_cols), :])
            for block in range(blocks)
        ]
        update = jnp.concatenate(updates, axis=1) * (1.0 / dp)

        @pl.when(mirrored)
        def _():
            new_ref[...] = masters_ref[...] - step_rate * flip(update)

        @pl.when(jnp.logical_not(mirrored))
        def _():
            new_ref[...] = masters_ref[...] - step_rate * update

        weights = new_ref[...].astype(bf16)
        for other in range(tensor):
            for k in range(ratio):
                product = jnp.dot(
                    feature_refs[other][k, :, pl.ds(pl.multiple_of(step * chunk, chunk), chunk)],
                    weights, preferred_element_type=f32)

                @pl.when(step == 0)
                def _():
                    products[other * ratio + k] = product

                @pl.when(step > 0)
                def _():
                    products[other * ratio + k] += product

        @pl.when(step == steps - 1)
        def _():
            base = (device // ratio) ^ rank
            for k in range(group):
                for cross in range(crosses):
                    target = cross * group + k
                    outs[k][cross] = products[
                        (base ^ (target // ratio)) * ratio + target % ratio
                    ].astype(bf16)

    def whole(*shape):
        return pl.BlockSpec(shape, lambda step, *scalars: (0,) * len(shape))

    def own_table(block):
        def index(step, *scalars):
            device = scalars[0][0]
            mirrored = device >= half_parts
            row = jnp.where(
                mirrored,
                (2 * half_parts - device) * steps - 1 - step,
                device * steps + step,
            )
            return (block * half_parts * steps + row, 0)

        return pl.BlockSpec((chunk, freqs), index)

    own = pl.BlockSpec((chunk, cols), lambda step, *scalars: (step, 0))
    return pl.pallas_call(
        kernel,
        name="apply",
        grid_spec=pltpu.PrefetchScalarGridSpec(
            num_scalar_prefetch=2,
            grid=(steps,),
            in_specs=[whole(*freq_rows.shape), own]
            + [own_table(block) for block in range(blocks)]
            + [pl.BlockSpec(memory_space=pltpu.VMEM)] * (group + tensor),
            out_specs=[own] + [whole(crosses, token_rows, cols)] * group,
            scratch_shapes=[
                pltpu.VMEM((cols, freqs), bf16),
                pltpu.VMEM((dp, token_rows, cols), f32),
            ],
        ),
        out_shape=[jax.ShapeDtypeStruct((own_rows, cols), f32)]
        + [jax.ShapeDtypeStruct((crosses, token_rows, cols), bf16)] * group,
        compiler_params=pltpu.CompilerParams(vmem_limit_bytes=vmem_bytes),
    )(*meta, freq_rows, masters, *[table] * blocks, *map(near, means), *map(near, features))


def near(value):
    return pltpu.with_memory_space_constraint(value, pltpu.VMEM)


def swap(value, axis, mask, size):
    return lax.ppermute(value, axis, [(k, k ^ mask) for k in range(size)])


def sum_low(values):
    total = values[0].astype(f32)
    for value in values[1:]:
        total = total + value.astype(f32)
    return total.astype(bf16)


def step(momentum, gradient, masters, tokens, freq_index):
    dp, tensor = lax.axis_size("dp"), lax.axis_size("tensor")
    group = min(4, dp)
    ratio = dp // tensor
    model_width = momentum.shape[1]
    device, rank = lax.axis_index("dp"), lax.axis_index("tensor")
    meta = (device.reshape(1).astype(jnp.int32), rank.reshape(1).astype(jnp.int32))
    freq_rows = freq_index

    pairs = [
        ((J * ratio + h) * tensor + j, (j * ratio + h) * tensor + J)
        for J in range(tensor) for h in range(ratio) for j in range(tensor)
    ]
    traded = lax.ppermute(tokens, ("dp", "tensor"), pairs)
    width = tokens.shape[1] // ratio

    coeff, *pieces, table = forward(momentum, gradient, freq_rows, meta, group)

    first = [swap(pieces[k], "dp", k, dp) for k in range(1, group)]

    residual = None

    def next_remain(part, residual):
        return remain(part, momentum, gradient, freq_rows, coeff, table, residual)

    def feature_piece(k):
        start = ((device % ratio) ^ k) * width
        return lax.dynamic_slice_in_dim(traded, start, width, axis=1)

    residual = next_remain(0, residual)
    summed = sum_low([pieces[0]] + first)
    summed = sum_low([summed] + [swap(summed, "dp", k * group, dp) for k in range(1, dp // group)])
    parts = [feature_piece(0)]
    for k in range(1, ratio):
        parts.append(swap(feature_piece(k), "dp", k, dp))
    residual = next_remain(1, residual)
    means = [summed] + [swap(summed, "dp", k, dp) for k in range(1, group)]
    features = {0: jnp.stack(parts)}
    mask = tensor // 2
    while mask > 0:
        for held in sorted(features):
            features[held ^ mask] = swap(features[held], "tensor", mask, tensor)
        mask //= 2
    residual = next_remain(2, residual)
    residual = next_remain(3, residual)
    new_masters, *partials = apply(
        masters, freq_rows, table, means, [features[k] for k in range(tensor)], meta, dp, tensor,
        group,
    )
    received = [swap(partials[k], "dp", k, dp) for k in range(1, group)]
    residual = next_remain(4, residual)
    residual = next_remain(5, residual)
    part = partials[0].astype(f32)
    for value in received:
        part = part + value.astype(f32)
    part_low = part.astype(bf16)
    total = part[0]
    for k in range(1, dp // group):
        total = total + swap(part_low[k], "dp", k * group, dp).astype(f32)
    projected = (total * model_width ** (-0.5)).astype(bf16)
    return (residual, new_masters, projected)


def solution(mesh):
    return jax.shard_map(
        step,
        mesh=mesh,
        in_specs=(
            P("dp", None, "tensor"),
            P("dp", None, "tensor"),
            P("dp", "tensor"),
            P("dp", "tensor"),
            P("tensor", None),
        ),
        out_specs=(P("dp", None, "tensor"), P("dp", "tensor"), P("dp", "tensor")),
        check_vma=False,
    )
```

```python
import math

import jax
import jax.numpy as jnp
from jax import lax
from jax.experimental import pallas as pl
from jax.experimental.pallas import tpu as pltpu
from jax.sharding import PartitionSpec as P


momentum_decay = 0.9
step_rate = 1.0
fine_rows = 64
forward_tile = 1024
remain_shares = (0, 4, 8, 12, 14, 16)
apply_rows = 1024
vmem_bytes = 20 * 1024 * 1024
f32 = jnp.float32
bf16 = jnp.bfloat16


def wrap(phase, period):
    return phase & (period - 1) if period & (period - 1) == 0 else phase % period


def sine_cosine(phase, model_width):
    shifted = phase + model_width // 2
    if model_width & (model_width - 1) == 0:
        quarter = shifted >> (model_width.bit_length() - 1)
    else:
        quarter = shifted // model_width
    x = (phase - quarter * model_width).astype(f32) * (math.pi / (2 * model_width))
    z = x * x
    sine = x + x * z * (-1.6666654611e-1 + z * (8.3321608736e-3 + z * -1.9515295891e-4))
    cosine = 1.0 - 0.5 * z + z * z * (
        4.166664568298827e-2 + z * (-1.388731625493765e-3 + z * 2.443315711809948e-5)
    )
    swapped = (quarter & 1) == 1
    cos_sign = (1 - ((quarter + 1) & 2)).astype(f32)
    sin_sign = (1 - (quarter & 2)).astype(f32)
    return (
        cos_sign * jnp.where(swapped, sine, cosine),
        sin_sign * jnp.where(swapped, cosine, sine),
    )


def fill_tables(frequency, coarse_cos, coarse_sin, fine_cos, fine_sin, twice, model_width):
    freqs = frequency.shape[1]
    digit = lax.broadcasted_iota(jnp.int32, (8, freqs), 0)
    scale = jnp.where(
        frequency == 0, math.sqrt(1.0 / model_width), math.sqrt(2.0 / model_width)
    ).astype(f32)

    def angles(multiplier):
        return sine_cosine(wrap(multiplier * frequency, 4 * model_width), model_width)

    def combine(high, low, cos_ref, sin_ref):
        for k in range(cos_ref.shape[0] // 8):
            rows = pl.ds(8 * k, 8)
            cosine, sine = high[0][k : k + 1], high[1][k : k + 1]
            cos_ref[rows, :] = cosine * low[0] - sine * low[1]
            sin_ref[rows, :] = sine * low[0] + cosine * low[1]

    cosine, sine = angles(2 * fine_rows * digit)
    twice[...] = 2.0 * jnp.broadcast_to(cosine[1:2], cosine.shape)
    combine(
        angles(16 * fine_rows * digit), (cosine * scale, sine * scale), coarse_cos, coarse_sin
    )
    combine(angles(16 * digit), angles(2 * digit + 1), fine_cos, fine_sin)


def fill_cosines(target, first_coarse, count, coarse_cos, coarse_sin, fine_cos, fine_sin, twice):
    for lane in range(0, target.shape[1], 128):
        lanes = pl.ds(lane, 128)
        cosine = fine_cos[:, lanes]
        sine = fine_sin[:, lanes]
        coarse_c = coarse_cos[pl.ds(first_coarse, 8), lanes]
        coarse_s = coarse_sin[pl.ds(first_coarse, 8), lanes]
        factor = jnp.broadcast_to(twice[0:1, lanes], cosine.shape)
        older = newer = None
        for k in range(count):
            if k < 2:
                value = coarse_c[k : k + 1] * cosine - coarse_s[k : k + 1] * sine
            else:
                value = factor * newer - older
            older, newer = newer, value
            target[pl.ds(k * fine_rows, fine_rows), lanes] = value.astype(bf16)


def flip(value):
    order = 7 - lax.broadcasted_iota(jnp.int32, (8, value.shape[1]), 0)
    pieces = [
        jnp.take_along_axis(value[row : row + 8], order, axis=0)
        for row in range(value.shape[0] - 8, -1, -8)
    ]
    return jnp.concatenate(pieces, axis=0)


def parity_sign(frequency):
    return (1 - 2 * (frequency & 1)).astype(f32)


def dot_tn(a, b):
    return lax.dot_general(a, b, (((0,), (0,)), ((), ())), preferred_element_type=f32)


def dot_nt(a, b):
    return lax.dot_general(a, b, (((1,), (1,)), ((), ())), preferred_element_type=f32)


def forward(momentum, gradient, freq_rows, meta, group):
    model_width = momentum.shape[1]
    blocks, freqs = freq_rows.shape
    cols = momentum.shape[2]
    block_cols = cols // blocks
    half = model_width // 2
    tile = min(forward_tile, half)
    steps = half // tile
    piece = cols // group

    def kernel(device_ref, rank_ref, freq, mom_a, mom_b, grad_a, grad_b, coeff, *rest):
        pieces = rest[:group]
        table, total, *tables = rest[group:]
        block, step = pl.program_id(0), pl.program_id(1)
        frequency = freq[0:1]
        for other in range(1, blocks):
            frequency = jnp.where(block == other, freq[other : other + 1], frequency)

        @pl.when(step == 0)
        def _():
            fill_tables(frequency, *tables, model_width)

        here = table.at[pl.ds(pl.multiple_of((block * steps + step) * tile, tile), tile), :]

        fill_cosines(
            here, pl.multiple_of(step * (tile // fine_rows), 8), tile // fine_rows, *tables
        )
        low_a = (momentum_decay * mom_a[0] + grad_a[0].astype(f32)).astype(bf16)
        low_b = flip(momentum_decay * mom_b[0] + grad_b[0].astype(f32)).astype(bf16)
        both = jnp.concatenate([low_a, low_b], axis=1)
        partial = dot_tn(both, here[...])

        @pl.when(step == 0)
        def _():
            total[...] = partial

        @pl.when(step > 0)
        def _():
            total[...] += partial

        @pl.when(step == steps - 1)
        def _():
            rows = pl.ds(pl.multiple_of(block * block_cols, block_cols), block_cols)
            coeff[rows, :] = (
                total[:block_cols] + parity_sign(frequency) * total[block_cols:]
            ).astype(bf16)

        @pl.when((step == steps - 1) & (block == blocks - 1))
        def _():
            for k in range(group):
                start = ((device_ref[0] % group) ^ k) * piece
                pieces[k][...] = coeff[pl.ds(pl.multiple_of(start, piece), piece), :]

    def whole(block, step, *scalars):
        return (0, 0)

    def rows(which):
        def index(block, step, *scalars):
            return (0, 2 * steps - 1 - step if which else step, block)

        return pl.BlockSpec((1, tile, block_cols), index)

    return pl.pallas_call(
        kernel,
        name="forward",
        grid_spec=pltpu.PrefetchScalarGridSpec(
            num_scalar_prefetch=2,
            grid=(blocks, steps),
            in_specs=[
                pl.BlockSpec((blocks, freqs), whole),
                rows(0), rows(1), rows(0), rows(1),
            ],
            out_specs=[pl.BlockSpec((cols, freqs), whole)]
            + [pl.BlockSpec((piece, freqs), whole)] * group
            + [pl.BlockSpec(memory_space=pltpu.VMEM)],
            scratch_shapes=[pltpu.VMEM((2 * block_cols, freqs), f32)]
            + [pltpu.VMEM((half // fine_rows, freqs), f32)] * 2
            + [pltpu.VMEM((fine_rows, freqs), f32)] * 2
            + [pltpu.VMEM((8, freqs), f32)],
        ),
        out_shape=[jax.ShapeDtypeStruct((cols, freqs), bf16)]
        + [jax.ShapeDtypeStruct((piece, freqs), bf16)] * group
        + [pltpu.VMEM((blocks * half, freqs), bf16)],
        compiler_params=pltpu.CompilerParams(vmem_limit_bytes=vmem_bytes),
    )(*meta, freq_rows, momentum, momentum, gradient, gradient)


def remain(part, momentum, gradient, freq_rows, coeff, table, previous):
    model_width = momentum.shape[1]
    block_cols = momentum.shape[2] // freq_rows.shape[0]
    blocks, freqs = freq_rows.shape
    half = model_width // 2
    tile = min(512 if blocks > 1 else 256, half)
    all_steps = half // tile
    begin, end = (all_steps * blocks * share // 16 for share in remain_shares[part : part + 2])
    column_block, first = divmod(begin, all_steps)
    steps = end - begin

    def kernel(freq, mom_a, mom_b, grad_a, grad_b, coeff_ref, table_ref, *rest):
        residual, _, both, buffer, sems = rest[-5:]
        step = pl.program_id(0)
        slot = step % 2

        def copies(at, where):
            lanes = pl.ds(column_block * block_cols, block_cols)
            return [
                pltpu.make_async_copy(
                    buffer.at[where, k], residual.at[0, pl.ds(start * tile, tile), lanes],
                    sems.at[where, k],
                )
                for k, start in enumerate((first + at, 2 * all_steps - 1 - first - at))
            ]

        @pl.when(step == 0)
        def _():
            both[:block_cols] = coeff_ref[...]
            both[block_cols:] = (coeff_ref[...].astype(f32) * parity_sign(freq[column_block : column_block + 1])).astype(bf16)

        at = (column_block * all_steps + first + step) * tile
        back = dot_nt(table_ref[pl.ds(pl.multiple_of(at, tile), tile), :], both[...])

        @pl.when(step >= 2)
        def _():
            for copy in copies(step - 2, slot):
                copy.wait()

        buffer[slot, 0] = (
            momentum_decay * mom_a[0] + grad_a[0].astype(f32) - back[:, :block_cols]
        )
        buffer[slot, 1] = (
            momentum_decay * mom_b[0] + grad_b[0].astype(f32) - flip(back[:, block_cols:])
        )
        for copy in copies(step, slot):
            copy.start()

        @pl.when(step == steps - 1)
        def _():
            if steps > 1:
                for copy in copies(step - 1, 1 - slot):
                    copy.wait()
            for copy in copies(step, slot):
                copy.wait()

    def rows(which):
        def index(step):
            at = first + step
            return (0, 2 * all_steps - 1 - at if which else at, column_block)

        return pl.BlockSpec((1, tile, block_cols), index)

    operands = [freq_rows, momentum, momentum, gradient, gradient, coeff, near(table)]
    specs = [
        pl.BlockSpec((blocks, freqs), lambda step: (0, 0)),
        rows(0), rows(1), rows(0), rows(1),
        pl.BlockSpec((block_cols, freqs), lambda step: (column_block, 0)),
        pl.BlockSpec(memory_space=pltpu.VMEM),
    ]
    aliases = {len(operands) - 1: 1}
    if previous is not None:
        aliases[len(operands)] = 0
        operands.append(previous)
        specs.append(pl.BlockSpec(memory_space=pl.ANY))
    return pl.pallas_call(
        kernel,
        grid=(steps,),
        in_specs=specs,
        out_specs=[pl.BlockSpec(memory_space=pl.ANY), pl.BlockSpec(memory_space=pltpu.VMEM)],
        scratch_shapes=[
            pltpu.VMEM((2 * block_cols, freqs), bf16),
            pltpu.VMEM((2, 2, tile, block_cols), f32),
            pltpu.SemaphoreType.DMA((2, 2)),
        ],
        out_shape=[
            jax.ShapeDtypeStruct(momentum.shape, f32), pltpu.VMEM(table.shape, table.dtype)
        ],
        input_output_aliases=aliases,
        compiler_params=pltpu.CompilerParams(vmem_limit_bytes=vmem_bytes),
    )(*operands)


def apply(masters, freq_rows, table, means, features, meta, dp, tensor, group):
    own_rows, cols = masters.shape
    blocks, freqs = freq_rows.shape
    block_cols = cols // blocks
    piece = cols // group
    ratio, token_rows, _ = features[0].shape
    half_parts = table.shape[0] // blocks // own_rows
    crosses = dp // group

    chunk = min(apply_rows, own_rows)
    steps = own_rows // chunk

    def kernel(device_ref, rank_ref, freq, masters_ref, *rest):
        table_ref, *rest = rest
        mean_refs = rest[:group]
        feature_refs = rest[group : group + tensor]
        new_ref, *outs, held, mean, products = rest[group + tensor :]
        device, rank = device_ref[0], rank_ref[0]
        step = pl.program_id(0)
        mirrored = device >= half_parts

        @pl.when(step == 0)
        def _():
            for k in range(group):
                start = ((device % group) ^ k) * piece
                mean[pl.ds(pl.multiple_of(start, piece), piece), :] = mean_refs[k][...]
            for block in range(blocks):
                rows = pl.ds(block * block_cols, block_cols)
                sign = jnp.where(mirrored, parity_sign(freq[block : block + 1]), 1.0)
                mean[rows, :] = (mean[rows, :].astype(f32) * sign).astype(bf16)

        row = jnp.where(
            mirrored, (2 * half_parts - device) * steps - 1 - step, device * steps + step
        )

        def own_table(block):
            start = (block * half_parts * steps + row) * chunk
            return table_ref[pl.ds(pl.multiple_of(start, chunk), chunk), :]

        updates = [
            dot_nt(own_table(block), mean[pl.ds(block * block_cols, block_cols), :])
            for block in range(blocks)
        ]
        update = jnp.concatenate(updates, axis=1) * (1.0 / dp)

        @pl.when(mirrored)
        def _():
            new_ref[...] = masters_ref[...] - step_rate * flip(update)

        @pl.when(jnp.logical_not(mirrored))
        def _():
            new_ref[...] = masters_ref[...] - step_rate * update

        weights = new_ref[...].astype(bf16)
        for other in range(tensor):
            for k in range(ratio):
                product = jnp.dot(
                    feature_refs[other][k, :, pl.ds(pl.multiple_of(step * chunk, chunk), chunk)],
                    weights, preferred_element_type=f32)

                @pl.when(step == 0)
                def _():
                    products[other * ratio + k] = product

                @pl.when(step > 0)
                def _():
                    products[other * ratio + k] += product

        @pl.when(step == steps - 1)
        def _():
            base = (device // ratio) ^ rank
            for k in range(group):
                for cross in range(crosses):
                    target = cross * group + k
                    outs[k][cross] = products[
                        (base ^ (target // ratio)) * ratio + target % ratio
                    ].astype(bf16)

    def whole(*shape):
        return pl.BlockSpec(shape, lambda step, *scalars: (0,) * len(shape))

    own = pl.BlockSpec((chunk, cols), lambda step, *scalars: (step, 0))
    return pl.pallas_call(
        kernel,
        name="apply",
        grid_spec=pltpu.PrefetchScalarGridSpec(
            num_scalar_prefetch=2,
            grid=(steps,),
            in_specs=[whole(*freq_rows.shape), own]
            + [pl.BlockSpec(memory_space=pltpu.VMEM)] * (1 + group + tensor),
            out_specs=[own] + [whole(crosses, token_rows, cols)] * group
            + [pl.BlockSpec(memory_space=pltpu.VMEM)],
            scratch_shapes=[
                pltpu.VMEM((cols, freqs), bf16),
                pltpu.VMEM((dp, token_rows, cols), f32),
            ],
        ),
        out_shape=[jax.ShapeDtypeStruct((own_rows, cols), f32)]
        + [jax.ShapeDtypeStruct((crosses, token_rows, cols), bf16)] * group
        + [pltpu.VMEM(table.shape, table.dtype)],
        input_output_aliases={4: 1 + group},
        compiler_params=pltpu.CompilerParams(vmem_limit_bytes=vmem_bytes),
    )(*meta, freq_rows, masters, near(table), *map(near, means), *map(near, features))


def pick(traded, device, ratio):
    rows, width = traded.shape[0], traded.shape[1] // ratio

    def kernel(device_ref, *refs):
        for k in range(ratio):
            refs[ratio + k][...] = refs[k][...]

    def piece(k):
        return pl.BlockSpec((rows, width), lambda step, scalar: (0, (scalar[0] % ratio) ^ k))

    return pl.pallas_call(
        kernel,
        name="pick",
        grid_spec=pltpu.PrefetchScalarGridSpec(
            num_scalar_prefetch=1,
            grid=(1,),
            in_specs=[piece(k) for k in range(ratio)],
            out_specs=[pl.BlockSpec((rows, width), lambda step, scalar: (0, 0))] * ratio,
        ),
        out_shape=[jax.ShapeDtypeStruct((rows, width), bf16)] * ratio,
        compiler_params=pltpu.CompilerParams(vmem_limit_bytes=vmem_bytes),
    )(device, *[pltpu.with_memory_space_constraint(traded, pltpu.HBM)] * ratio)


def near(value):
    return pltpu.with_memory_space_constraint(value, pltpu.VMEM)


def swap(value, axis, mask, size):
    return lax.ppermute(value, axis, [(k, k ^ mask) for k in range(size)])


def sum_low(values):
    total = values[0].astype(f32)
    for value in values[1:]:
        total = total + value.astype(f32)
    return total.astype(bf16)


def step(momentum, gradient, masters, tokens, freq_index):
    dp, tensor = lax.axis_size("dp"), lax.axis_size("tensor")
    group = min(4, dp)
    ratio = dp // tensor
    model_width = momentum.shape[1]
    device, rank = lax.axis_index("dp"), lax.axis_index("tensor")
    meta = (device.reshape(1).astype(jnp.int32), rank.reshape(1).astype(jnp.int32))
    freq_rows = freq_index

    momentum = pltpu.with_memory_space_constraint(momentum, pltpu.HBM)
    gradient = pltpu.with_memory_space_constraint(gradient, pltpu.HBM)

    pairs = [
        ((J * ratio + h) * tensor + j, (j * ratio + h) * tensor + J)
        for J in range(tensor) for h in range(ratio) for j in range(tensor)
    ]
    traded = lax.ppermute(tokens, ("dp", "tensor"), pairs)

    coeff, *pieces, table = forward(momentum, gradient, freq_rows, meta, group)

    first = [swap(pieces[k], "dp", k, dp) for k in range(1, group)]

    residual = None

    def next_remain(part, residual, table):
        return remain(part, momentum, gradient, freq_rows, coeff, table, residual)

    summed = sum_low([pieces[0]] + first)
    summed = sum_low([summed] + [swap(summed, "dp", k * group, dp) for k in range(1, dp // group)])
    chosen = pick(traded, meta[0], ratio)
    parts = [chosen[0]]
    for k in range(1, ratio):
        parts.append(swap(chosen[k], "dp", k, dp))
    residual, table = next_remain(0, residual, table)
    means = [summed] + [swap(summed, "dp", k, dp) for k in range(1, group)]
    features = {0: jnp.stack(parts)}
    mask = tensor // 2
    while mask > 0:
        for held in sorted(features):
            features[held ^ mask] = swap(features[held], "tensor", mask, tensor)
        mask //= 2
    residual, table = next_remain(1, residual, table)
    residual, table = next_remain(2, residual, table)
    new_masters, *partials, table = apply(
        masters, freq_rows, table, means, [features[k] for k in range(tensor)], meta, dp, tensor,
        group,
    )
    received = [swap(partials[k], "dp", k, dp) for k in range(1, group)]
    residual, table = next_remain(3, residual, table)
    residual, table = next_remain(4, residual, table)
    part = partials[0].astype(f32)
    for value in received:
        part = part + value.astype(f32)
    part_low = part.astype(bf16)
    total = part[0]
    for k in range(1, dp // group):
        total = total + swap(part_low[k], "dp", k * group, dp).astype(f32)
    projected = (total * model_width ** (-0.5)).astype(bf16)
    return (residual, new_masters, projected)


def solution(mesh):
    return jax.shard_map(
        step,
        mesh=mesh,
        in_specs=(
            P("dp", None, "tensor"),
            P("dp", None, "tensor"),
            P("dp", "tensor"),
            P("dp", "tensor"),
            P("tensor", None),
        ),
        out_specs=(P("dp", None, "tensor"), P("dp", "tensor"), P("dp", "tensor")),
        check_vma=False,
    )
```
